32 devices in a mesh: section: 4 (over x, core), ctx: 8 (over z, y).
Axes of the slice: x: 2, y: 2, z: 4, core: 2. Of those that a mesh axis runs over, the one named last changes fastest.
Arguments:
- tokens: bfloat16 [6144, 8192], P(('section', 'ctx')), may hold values from -60 to 60
- norm_gain: float32 [1, 2, 8192], replicated, may hold values from 0.1 to 1.9
- feat_taps: float32 [1, 2, 3, 3, 8192], replicated, may hold values from -3.5 to 3.5
- se_taps: float32 [1, 7, 8192], replicated, may hold values from -2 to 2
- mr_taps: bfloat16 [1, 128, 512], replicated, may hold values from -0.5 to 0.5
Outputs:
- final: bfloat16 [6144, 8192], P(('section', 'ctx'))
The draws below stay inside these ranges and needn't reach their ends.
All inputs are finite; a program needn't handle non-finite values.
Results may differ from the reference program's by a relative error of at most 0.0089.
Values may be sent and summed in bfloat16 or wider, within the bound.
A program may use at most 192 MiB of HBM per device.

```python
import jax
import jax.numpy as jnp
from jax import lax

D = 8192
GROUPS = 512
FEAT = 3
SE_TAPS = 7
MR_TAPS = 128
LAYERS = 1
SEQ = 6144


def draw_tokens(key, part):
    key_base, key_rows, key_cols = jax.random.split(key, 3)
    base = jax.random.truncated_normal(key_base, -6.0, 6.0, (SEQ, D), jnp.float32)
    row_scale = jnp.exp(jax.random.uniform(key_rows, (SEQ, 1), jnp.float32, -1.15, 1.15))
    col_scale = jnp.exp(jax.random.uniform(key_cols, (1, D), jnp.float32, -1.15, 1.15))
    return (base * row_scale * col_scale).astype(jnp.bfloat16)


def noise(own_key, shape, spread, limit, held_as=jnp.bfloat16):
    return jnp.clip(spread * jax.random.normal(own_key, shape, jnp.float32), -limit, limit).astype(held_as)


def setup_inputs(seed: int = 0) -> dict:
    keys = jax.random.split(jax.random.key(seed), 6)
    tokens = draw_tokens(jax.random.fold_in(keys[5], 71), 0)
    norm_gain = jnp.clip(1.0 + 0.18 * jax.random.normal(keys[1], (LAYERS, 2, D), jnp.float32), 0.1, 1.9)
    feat_taps = noise(keys[2], (LAYERS, 2, 3, FEAT, D), FEAT ** -0.5, 3.5, jnp.float32)
    se_taps = noise(keys[3], (LAYERS, SE_TAPS, D), SE_TAPS ** -0.5, 2.0, jnp.float32)
    mr_taps = noise(keys[4], (LAYERS, MR_TAPS, GROUPS), MR_TAPS ** -0.5, 0.5)
    return {"tokens": tokens, "norm_gain": norm_gain, "feat_taps": feat_taps, "se_taps": se_taps, "mr_taps": mr_taps}


def normalize(hidden, gain):
    values = hidden.astype(jnp.float32)
    mean_square = lax.optimization_barrier(jnp.mean(values * values, axis=-1, keepdims=True))
    return values * lax.rsqrt(mean_square + 1e-06) * gain

def delay(values, lag_rows):
    return jnp.pad(values, ((lag_rows, 0), (0, 0)))[:values.shape[0]]

def short_filter(product, filter_taps):
    values = product.astype(jnp.float32)
    summed = filter_taps[0] * values
    for i in range(1, filter_taps.shape[0]):
        summed = summed + filter_taps[i] * delay(values, i)
    return summed

def long_filter(product, filter_taps):
    values = product.astype(jnp.float32)
    row_total = values.shape[0]
    tap_count = filter_taps.shape[0]
    factor = values.shape[1] // filter_taps.shape[1]
    full_taps = jnp.repeat(filter_taps.astype(jnp.float32), factor, axis=1)
    padded = jnp.pad(values, ((tap_count - 1, 0), (0, 0)))

    def accumulate(i, summed):
        window_rows = lax.dynamic_slice_in_dim(padded, tap_count - 1 - i, row_total, 0)
        tap_row = lax.dynamic_index_in_dim(full_taps, i, 0, keepdims=False)
        return summed + tap_row * window_rows
    return lax.fori_loop(0, tap_count, accumulate, jnp.zeros(values.shape, jnp.float32))

def apply_operator(hidden, gain, feature_taps, filter_fn):
    scaled = normalize(hidden, gain)
    streams = []
    for j in range(3):
        summed = feature_taps[j, 0] * scaled
        for i in range(1, feature_taps.shape[1]):
            summed = summed + feature_taps[j, i] * delay(scaled, i)
        streams.append(summed)
    product = (streams[1] * streams[2]).astype(jnp.bfloat16)
    filtered = filter_fn(product)
    return (hidden.astype(jnp.float32) + streams[0] * filtered).astype(jnp.bfloat16)

def reference(tokens, norm_gain, feat_taps, se_taps, mr_taps):
    hidden = tokens
    for layer in range(LAYERS):
        short_taps = se_taps[layer]
        long_taps = mr_taps[layer]
        hidden = apply_operator(hidden, norm_gain[layer, 0], feat_taps[layer, 0], lambda p: short_filter(p, short_taps))
        hidden = apply_operator(hidden, norm_gain[layer, 1], feat_taps[layer, 1], lambda p: long_filter(p, long_taps))
    return hidden
```

```python
import functools

import jax
import jax.numpy as jnp
from jax import lax
from jax.experimental import pallas as pl
from jax.experimental.pallas import tpu as pltpu
from jax.sharding import PartitionSpec as P

F32 = jnp.float32
BF16 = jnp.bfloat16
LANES = 128
WIDE = 256
CHUNKS = 4


def from_behind(x, axis, by):
    length = lax.axis_size(axis)
    pairs = [(i, i + by) for i in range(length) if 0 <= i + by < length]
    return lax.ppermute(x, axis, pairs)


def lanes_of(c, width=LANES):
    return pl.ds(pl.multiple_of(c * width, width), width)


def write_scale(total, scale_ref, channels):
    mean = jnp.sum(total, axis=-1, keepdims=True) * (1.0 / channels)
    scale_ref[...] = jnp.broadcast_to(lax.rsqrt(mean + 1e-06), scale_ref.shape)


def square_sums(x_ref, blocks):
    def add(c, total):
        v = x_ref[:, lanes_of(c)].astype(F32)
        return total + v * v

    return lax.fori_loop(0, blocks, add, jnp.zeros((x_ref.shape[0], LANES), F32))


def stream(z_ref, taps, rows):
    feat = taps.shape[0]
    total = taps[0:1] * z_ref[8 : 8 + rows]
    for i in range(1, feat):
        total = total + taps[i : i + 1] * z_ref[8 - i : 8 - i + rows]
    return total


def short_block(c, x_ref, scale_ref, z_ref, w_ref, gain_ref, feat_ref, taps_ref):
    rows = x_ref.shape[0]
    cs = lanes_of(c)
    x = x_ref[:, cs].astype(F32)
    z_ref[8:] = x * scale_ref[...] * gain_ref[:, cs]
    u1 = stream(z_ref, feat_ref[1, :, cs], rows)
    u2 = stream(z_ref, feat_ref[2, :, cs], rows)
    w_ref[8:] = (u1 * u2).astype(BF16).astype(F32)
    f = stream(w_ref, taps_ref[:, cs], rows)
    return x + stream(z_ref, feat_ref[0, :, cs], rows) * f


def tail_kernel(x_ref, gain1_ref, feat1_ref, taps_ref, gain2_ref, feat2_ref, out_ref,
                h_ref, s1_ref, s2_ref, z_ref, w_ref, z2_ref, sum_ref):
    rows, channels = x_ref.shape
    blocks = channels // LANES
    z_ref[...] = jnp.zeros_like(z_ref)
    w_ref[...] = jnp.zeros_like(w_ref)
    sum_ref[...] = jnp.zeros_like(sum_ref)
    write_scale(square_sums(x_ref, blocks), s1_ref, channels)

    @pl.loop(0, blocks)
    def _(c):
        h = short_block(c, x_ref, s1_ref, z_ref, w_ref, gain1_ref, feat1_ref, taps_ref)
        h = h.astype(BF16)
        h_ref[:, lanes_of(c)] = h
        hf = h.astype(F32)
        sum_ref[...] += hf * hf

    write_scale(sum_ref[...], s2_ref, channels)
    sent = out_ref.shape[0]

    @pl.loop(0, blocks)
    def _(c):
        cs = lanes_of(c)
        z2_ref[8:] = h_ref[:, cs].astype(F32) * s2_ref[...] * gain2_ref[:, cs]
        first = rows - sent
        u1 = stream(z2_ref.at[first:], feat2_ref[1, :, cs], sent)
        u2 = stream(z2_ref.at[first:], feat2_ref[2, :, cs], sent)
        out_ref[:, cs] = (u1 * u2).astype(BF16)


def local_kernel(lead_ref, x_ref, gain1_ref, feat1_ref, taps_ref, gain2_ref, feat2_ref,
                 h_out, u_out, w_out, x_all, h_ref, s1_ref, s2_ref, z_ref, w_ref, z2_ref, sum_ref):
    lead = lead_ref.shape[0]
    rows, channels = x_all.shape
    blocks = channels // LANES
    x_all[:lead] = lead_ref[...]
    x_all[lead:] = x_ref[...]
    z_ref[...] = jnp.zeros_like(z_ref)
    w_ref[...] = jnp.zeros_like(w_ref)
    sum_ref[...] = jnp.zeros_like(sum_ref)
    write_scale(square_sums(x_all, blocks), s1_ref, channels)

    @pl.loop(0, blocks)
    def _(c):
        h = short_block(c, x_all, s1_ref, z_ref, w_ref, gain1_ref, feat1_ref, taps_ref)
        h = h.astype(BF16)
        h_ref[:, lanes_of(c)] = h
        h_out[:, lanes_of(c)] = h[lead:]
        hf = h.astype(F32)
        sum_ref[...] += hf * hf

    write_scale(sum_ref[...], s2_ref, channels)
    kept = rows - lead

    @pl.loop(0, blocks)
    def _(c):
        cs = lanes_of(c)
        z2_ref[8:] = h_ref[:, cs].astype(F32) * s2_ref[...] * gain2_ref[:, cs]
        z = z2_ref.at[lead:]
        u1 = stream(z, feat2_ref[1, :, cs], kept)
        u2 = stream(z, feat2_ref[2, :, cs], kept)
        w_out[:, cs] = (u1 * u2).astype(BF16)
        u_out[:, cs] = stream(z, feat2_ref[0, :, cs], kept)


def long_kernel(tap_count, per_group, base_ref, halo_ref, w_ref, u_ref, h_ref, *rest):
    out_ref, table, window = rest[-3:]
    kept, width = w_ref.shape
    groups = width // per_group
    for g in range(groups):
        row = jnp.broadcast_to(base_ref[g : g + 1, :], (tap_count, 2 * tap_count))
        rolled = pltpu.roll(row, 0, 1, stride=1, stride_axis=0)
        table[g * tap_count : (g + 1) * tap_count] = rolled.astype(BF16)
    lane_group = lax.broadcasted_iota(jnp.int32, (tap_count, width), 1) // per_group
    window[:tap_count] = halo_ref[...]
    window[tap_count : tap_count + kept] = w_ref[...]
    window[tap_count + kept :] = jnp.zeros((window.shape[0] - tap_count - kept, width), BF16)
    start = 0
    while start < kept:
        count = min(tap_count, kept - start)
        product = jnp.dot(table[...], window[start : start + 2 * tap_count],
                          preferred_element_type=F32)
        f = product[0:count]
        for g in range(1, groups):
            f = jnp.where(lane_group[:count] == g,
                          product[g * tap_count : g * tap_count + count], f)
        part = slice(start, start + count)
        out_ref[part] = (h_ref[part].astype(F32) + u_ref[part] * f).astype(BF16)
        start += count


def whole():
    return pl.BlockSpec(memory_space=pltpu.VMEM)


def on_device(tokens, norm_gain, feat_taps, se_taps, mr_taps):
    rows, channels = tokens.shape
    tap_count, group_count = mr_taps.shape[1:]
    per_group = channels // group_count
    gain1, gain2 = norm_gain[0, 0:1], norm_gain[0, 1:2]
    feat1, feat2 = feat_taps[0, 0], feat_taps[0, 1]
    short = se_taps[0]
    lead = 16
    tail = tap_count + 16
    params = pltpu.CompilerParams(vmem_limit_bytes=60 * 1024 * 1024)
    before = from_behind(tokens[-lead:], ("section", "ctx"), 1)

    def scratch(count):
        return [
            pltpu.VMEM((count, channels), BF16),
            pltpu.VMEM((count, LANES), F32),
            pltpu.VMEM((count, LANES), F32),
            pltpu.VMEM((8 + count, LANES), F32),
            pltpu.VMEM((8 + count, LANES), F32),
            pltpu.VMEM((8 + count, LANES), F32),
            pltpu.VMEM((count, LANES), F32),
        ]

    sent = pl.pallas_call(
        tail_kernel,
        out_shape=jax.ShapeDtypeStruct((tap_count, channels), BF16),
        in_specs=[whole()] * 6,
        out_specs=whole(),
        scratch_shapes=scratch(tail),
        compiler_params=params,
        name="tail",
    )(tokens[-tail:], gain1, feat1, short, gain2, feat2)
    part = channels // CHUNKS
    halos = [from_behind(sent[:, k * part : (k + 1) * part], ("section", "ctx"), 1)
             for k in range(CHUNKS)]
    h, u, w = pl.pallas_call(
        local_kernel,
        out_shape=(
            jax.ShapeDtypeStruct((rows, channels), BF16),
            jax.ShapeDtypeStruct((rows, channels), F32),
            jax.ShapeDtypeStruct((rows, channels), BF16),
        ),
        in_specs=[whole()] * 7,
        out_specs=(whole(),) * 3,
        scratch_shapes=[pltpu.VMEM((rows + lead, channels), BF16)] + scratch(rows + lead),
        compiler_params=params,
        name="local",
    )(before, tokens, gain1, feat1, short, gain2, feat2)
    base = jnp.pad(mr_taps[0].astype(F32).T[:, ::-1], ((0, 0), (1, tap_count - 1)))
    out = None
    window_rows = -(-rows // tap_count) * tap_count + tap_count
    for k in range(CHUNKS):
        first = k * part // WIDE
        here = lambda i, first=first: (0, first + i)
        operands = [base, halos[k], w, u, h]
        specs = [
            pl.BlockSpec((WIDE // per_group, 2 * tap_count), lambda i, first=first: (first + i, 0)),
            pl.BlockSpec((tap_count, WIDE), lambda i: (0, i)),
            pl.BlockSpec((rows, WIDE), here),
            pl.BlockSpec((rows, WIDE), here),
            pl.BlockSpec((rows, WIDE), here),
        ]
        aliases = {}
        if out is not None:
            operands.append(out)
            specs.append(pl.BlockSpec(memory_space=pl.ANY))
            aliases = {5: 0}
        out = pl.pallas_call(
            functools.partial(long_kernel, tap_count, per_group),
            out_shape=jax.ShapeDtypeStruct((rows, channels), BF16),
            grid=(part // WIDE,),
            in_specs=specs,
            out_specs=pl.BlockSpec((rows, WIDE), here),
            scratch_shapes=[
                pltpu.VMEM((WIDE // per_group * tap_count, 2 * tap_count), BF16),
                pltpu.VMEM((window_rows, WIDE), BF16),
            ],
            input_output_aliases=aliases,
            compiler_params=params,
            name="long",
        )(*operands)
    return out


def solution(mesh):
    placed = (P(("section", "ctx"), None), P(), P(), P(), P())
    return jax.shard_map(
        on_device,
        mesh=mesh,
        in_specs=placed,
        out_specs=P(("section", "ctx"), None),
        check_vma=False,
    )
```

```python
import functools

import jax
import jax.numpy as jnp
from jax import lax
from jax.experimental import pallas as pl
from jax.experimental.pallas import tpu as pltpu
from jax.sharding import PartitionSpec as P

F32 = jnp.float32
BF16 = jnp.bfloat16
LANES = 128
CHUNKS = 8
LEAD = 16
MESH = pl.DeviceIdType.MESH


def lanes_of(c, width=LANES):
    return pl.ds(pl.multiple_of(c * width, width), width)


def row_scale(total, channels):
    mean = jnp.sum(total, axis=-1, keepdims=True) * (1.0 / channels)
    return jnp.broadcast_to(lax.rsqrt(mean + 1e-06), total.shape)


def square_sums(read, rows, blocks):
    def add(c, total):
        v = read(c).astype(F32)
        return total + v * v

    return lax.fori_loop(0, blocks, add, jnp.zeros((rows, LANES), F32))


def stream(z_ref, taps, first, rows):
    total = taps[0:1] * z_ref[8 + first : 8 + first + rows]
    for i in range(1, taps.shape[0]):
        total = total + taps[i : i + 1] * z_ref[8 + first - i : 8 + first - i + rows]
    return total


def pieces(rows, most=48):
    return [(first, min(most, rows - first)) for first in range(0, rows, most)]


def short_rows(read, rows, start, blocks, channels, gain_ref, feat_ref, taps_ref, h_ref,
               scale_ref, z_ref, w_ref, s_ref, sum_ref):
    s_ref[:rows] = row_scale(square_sums(read, rows, blocks), channels)
    sum_ref[:rows] = jnp.zeros((rows, LANES), F32)

    @pl.loop(0, blocks)
    def _(c):
        cs = lanes_of(c)
        gain = gain_ref[0, 0:1, cs]
        taps = [feat_ref[0, 0, j, :, cs] * gain for j in range(3)]
        short = taps_ref[0, :, cs]
        z_ref[8 : 8 + rows] = read(c).astype(F32) * s_ref[:rows]
        for first, count in pieces(rows):
            u1 = stream(z_ref, taps[1], first, count)
            u2 = stream(z_ref, taps[2], first, count)
            w_ref[8 + first : 8 + first + count] = (u1 * u2).astype(BF16).astype(F32)
        for first, count in pieces(rows):
            f = stream(w_ref, short, first, count)
            u0 = stream(z_ref, taps[0], first, count)
            h_ref[start + first : start + first + count, cs] = u0 * f
        h = (h_ref[start : start + rows, cs] + read(c).astype(F32)).astype(BF16).astype(F32)
        h_ref[start : start + rows, cs] = h
        sum_ref[:rows] += h * h

    scale_ref[start : start + rows] = row_scale(sum_ref[:rows], channels)


def kernel(axes, x_ref, gain_ref, feat_ref, taps_ref, mr_ref, out_ref,
           lead_ref, win_ref, h_ref, u_ref, table_ref, base_ref, rhs_ref, scale_ref, z_ref, w_ref,
           s_ref, sum_ref, lead_sems, send_sems, recv_sems):
    rows, channels = x_ref.shape
    tap_count, group_count = mr_ref.shape[1:]
    per_group = channels // group_count
    groups = LANES // per_group
    half = rows // 2
    blocks = channels // LANES
    part = channels // CHUNKS
    outer, inner = axes
    inner_size = lax.axis_size(inner)
    count = lax.axis_size(outer) * inner_size
    me = lax.axis_index(outer) * inner_size + lax.axis_index(inner)
    behind, ahead = me - 1, me + 1
    has_behind, has_ahead = me > 0, me < count - 1

    def place(index):
        return (index // inner_size, index % inner_size)

    barrier = pltpu.get_barrier_semaphore()

    @pl.when(has_behind)
    def _():
        pl.semaphore_signal(barrier, inc=1, device_id=place(behind), device_id_type=MESH)

    @pl.when(has_ahead)
    def _():
        pl.semaphore_signal(barrier, inc=1, device_id=place(ahead), device_id_type=MESH)

    peers = has_behind.astype(jnp.int32) + has_ahead.astype(jnp.int32)
    pl.semaphore_wait(barrier, peers)

    def lead_copy():
        return pltpu.make_async_remote_copy(
            src_ref=x_ref.at[pl.ds(rows - LEAD, LEAD)], dst_ref=lead_ref,
            send_sem=lead_sems.at[0], recv_sem=lead_sems.at[1],
            device_id=place(ahead), device_id_type=MESH)

    def part_copy(k):
        cs = lanes_of(k, part)
        return pltpu.make_async_remote_copy(
            src_ref=win_ref.at[pl.ds(rows, tap_count), cs],
            dst_ref=win_ref.at[pl.ds(0, tap_count), cs],
            send_sem=send_sems.at[k], recv_sem=recv_sems.at[k],
            device_id=place(ahead), device_id_type=MESH)

    @pl.when(has_ahead)
    def _():
        lead_copy().start()

    z_ref[...] = jnp.zeros_like(z_ref)
    w_ref[...] = jnp.zeros_like(w_ref)
    share = (blocks, channels, gain_ref, feat_ref, taps_ref, h_ref, scale_ref, z_ref, w_ref,
             s_ref, sum_ref)

    tail = tap_count + LEAD
    first_tail = rows - tail
    short_rows(lambda c: x_ref[first_tail:, lanes_of(c)], tail, LEAD + first_tail, *share)
    first_sent = rows - tap_count

    @pl.loop(0, CHUNKS)
    def _(k):
        @pl.loop(0, blocks // CHUNKS)
        def _(b):
            cs = lanes_of(k * (blocks // CHUNKS) + b)
            gain = gain_ref[0, 1:2, cs]
            taps = [feat_ref[0, 1, j, :, cs] * gain for j in range(3)]
            n = tap_count + 8
            top = LEAD + first_sent - 8
            z_ref[0:n] = h_ref[top : top + n, cs] * scale_ref[top : top + n]
            for first, size in pieces(tap_count):
                u1 = stream(z_ref, taps[1], first, size)
                u2 = stream(z_ref, taps[2], first, size)
                win_ref[rows + first : rows + first + size, cs] = (u1 * u2).astype(BF16)

        @pl.when(has_ahead & (k > 0))
        def _():
            part_copy(k - 1).start()

    spread = 2 * tap_count
    at_tap = lax.broadcasted_iota(jnp.int32, (tap_count, spread), 0)
    at_lag = lax.broadcasted_iota(jnp.int32, (tap_count, spread), 1)
    flip = jnp.where(at_tap + at_lag == tap_count, 1.0, 0.0).astype(BF16)
    base_ref[...] = lax.dot_general(mr_ref[0], flip, (((0,), (0,)), ((), ())),
                                    preferred_element_type=F32)
    rhs_ref[...] = jnp.zeros_like(rhs_ref)

    @pl.when(has_ahead)
    def _():
        part_copy(CHUNKS - 1).start()

    @pl.when(has_behind)
    def _():
        lead_copy().wait_recv()

    @pl.when(jnp.logical_not(has_behind))
    def _():
        lead_ref[...] = jnp.zeros_like(lead_ref)
        win_ref[:tap_count] = jnp.zeros((tap_count, channels), BF16)

    head = LEAD + first_sent
    z_ref[0:8] = jnp.zeros((8, LANES), F32)
    short_rows(
        lambda c: jnp.concatenate([lead_ref[:, lanes_of(c)], x_ref[:first_sent, lanes_of(c)]], axis=0),
        head, 0, *share)

    @pl.loop(0, blocks)
    def _(c):
        cs = lanes_of(c)
        gain = gain_ref[0, 1:2, cs]
        taps = [feat_ref[0, 1, j, :, cs] * gain for j in range(3)]
        z_ref[0 : rows + 8] = h_ref[LEAD - 8 :, cs] * scale_ref[LEAD - 8 :]
        for first, size in pieces(first_sent):
            u1 = stream(z_ref, taps[1], first, size)
            u2 = stream(z_ref, taps[2], first, size)
            win_ref[tap_count + first : tap_count + first + size, cs] = (u1 * u2).astype(BF16)
        for first, size in pieces(rows):
            u_ref[first : first + size, cs] = stream(z_ref, taps[0], first, size)

    @pl.loop(0, blocks)
    def _(c):
        lags = base_ref[pl.ds(pl.multiple_of(c * groups, groups), groups), :]
        for g in range(groups):
            row = jnp.broadcast_to(lags[g : g + 1], (half, spread))
            rolled = pltpu.roll(row, 0, 1, stride=1, stride_axis=0)
            table_ref[c, g * half : (g + 1) * half] = rolled.astype(BF16)

    lane_group = lax.broadcasted_iota(jnp.int32, (half, LANES), 1) // per_group
    reach = half + tap_count

    @pl.loop(0, CHUNKS)
    def _(k):
        @pl.when(has_behind)
        def _():
            part_copy(k).wait_recv()

        @pl.loop(0, blocks // CHUNKS)
        def _(b):
            c = k * (blocks // CHUNKS) + b
            cs = lanes_of(c)
            rhs_ref[:reach, :LANES] = win_ref[:reach, cs]
            rhs_ref[:reach, LANES:] = win_ref[half : half + reach, cs]
            product = jnp.dot(table_ref[c], rhs_ref[...], preferred_element_type=F32)
            for side in range(2):
                ls = slice(side * LANES, (side + 1) * LANES)
                f = product[0:half, ls]
                for g in range(1, groups):
                    f = jnp.where(lane_group == g, product[g * half : (g + 1) * half, ls], f)
                rs = slice(side * half, (side + 1) * half)
                hs = slice(LEAD + side * half, LEAD + (side + 1) * half)
                out_ref[rs, cs] = (h_ref[hs, cs] + u_ref[rs, cs] * f).astype(BF16)

    @pl.when(has_ahead)
    def _():
        lead_copy().wait_send()

        @pl.loop(0, CHUNKS)
        def _(k):
            part_copy(k).wait_send()


def on_device(axes, tokens, norm_gain, feat_taps, se_taps, mr_taps):
    rows, channels = tokens.shape
    tap_count, group_count = mr_taps.shape[1:]
    groups = LANES * group_count // channels
    blocks = channels // LANES
    spread = 2 * tap_count
    return pl.pallas_call(
        functools.partial(kernel, axes),
        out_shape=jax.ShapeDtypeStruct((rows, channels), BF16),
        in_specs=[pl.BlockSpec(memory_space=pltpu.VMEM)] * 5,
        out_specs=pl.BlockSpec(memory_space=pltpu.VMEM),
        scratch_shapes=[
            pltpu.VMEM((LEAD, channels), BF16),
            pltpu.VMEM((tap_count + rows, channels), BF16),
            pltpu.VMEM((LEAD + rows, channels), F32),
            pltpu.VMEM((rows, channels), F32),
            pltpu.VMEM((blocks, groups * rows // 2, spread), BF16),
            pltpu.VMEM((group_count, spread), F32),
            pltpu.VMEM((spread, 2 * LANES), BF16),
            pltpu.VMEM((LEAD + rows, LANES), F32),
            pltpu.VMEM((LEAD + rows, LANES), F32),
            pltpu.VMEM((LEAD + rows, LANES), F32),
            pltpu.VMEM((LEAD + rows, LANES), F32),
            pltpu.VMEM((LEAD + rows, LANES), F32),
            pltpu.SemaphoreType.DMA((2,)),
            pltpu.SemaphoreType.DMA((CHUNKS,)),
            pltpu.SemaphoreType.DMA((CHUNKS,)),
        ],
        compiler_params=pltpu.CompilerParams(
            collective_id=0, has_side_effects=True, vmem_limit_bytes=67043328),
        name="pair",
    )(tokens, norm_gain, feat_taps, se_taps, mr_taps)


def solution(mesh):
    axes = tuple(mesh.axis_names)
    placed = (P(axes, None), P(), P(), P(), P())
    return jax.shard_map(
        functools.partial(on_device, axes),
        mesh=mesh,
        in_specs=placed,
        out_specs=P(axes, None),
        check_vma=False,
    )
```

```python
import functools

import jax
import jax.numpy as jnp
from jax import lax
from jax.experimental import pallas as pl
from jax.experimental.pallas import tpu as pltpu
from jax.sharding import PartitionSpec as P

F32 = jnp.float32
BF16 = jnp.bfloat16
LANES = 128
CHUNKS = 16
EARLY = 4
STEP = 4
LEAD = 16
MESH = pl.DeviceIdType.MESH


def lanes_of(c, width=LANES):
    return pl.ds(pl.multiple_of(c * width, width), width)


def row_scale(total, channels):
    mean = jnp.sum(total, axis=-1, keepdims=True) * (1.0 / channels)
    return jnp.broadcast_to(lax.rsqrt(mean + 1e-06), total.shape)


def square_sums(read, rows, blocks):
    def add(c, total):
        v = read(c).astype(F32)
        return total + v * v

    return lax.fori_loop(0, blocks, add, jnp.zeros((rows, LANES), F32))


def stream(z_ref, taps, first, rows):
    total = taps[0] * z_ref[8 + first : 8 + first + rows]
    for i in range(1, len(taps)):
        total = total + taps[i] * z_ref[8 + first - i : 8 + first - i + rows]
    return total


def feat_rows(feat_ref, o, gain, cs):
    streams, feat = feat_ref.shape[1:3]
    return [[feat_ref[0, j, i, o : o + 1, cs] * gain for i in range(feat)] for j in range(streams)]


def pieces(rows, most=48):
    return [(first, min(most, rows - first)) for first in range(0, rows, most)]


def short_block(c, read, rows, start, gain_ref, feat_ref, taps_ref, h_ref, z_ref, w_ref, s_ref, sum_ref):
    cs = lanes_of(c)
    gain = gain_ref[0, 0:1, cs]
    taps = feat_rows(feat_ref, 0, gain, cs)
    short = [taps_ref[i, 0:1, cs] for i in range(taps_ref.shape[0])]
    z_ref[8 : 8 + rows] = read(c).astype(F32) * s_ref[:rows]
    for first, count in pieces(rows):
        u1 = stream(z_ref, taps[1], first, count)
        u2 = stream(z_ref, taps[2], first, count)
        w_ref[8 + first : 8 + first + count] = (u1 * u2).astype(BF16).astype(F32)
    for first, count in pieces(rows):
        f = stream(w_ref, short, first, count)
        u0 = stream(z_ref, taps[0], first, count)
        h_ref[start + first : start + first + count, cs] = u0 * f
    h = (h_ref[start : start + rows, cs] + read(c).astype(F32)).astype(BF16).astype(F32)
    h_ref[start : start + rows, cs] = h
    sum_ref[:rows] += h * h


def kernel(axes, x_ref, gain_ref, feat_ref, taps_ref, mr_ref, out_ref,
           lead_ref, win_ref, h_ref, u_ref, table_ref, base_ref, rhs_ref, scale_ref, z_ref, w_ref,
           s_ref, sum_ref, tell_ref, told_ref, give_ref, got_ref, lead_sems, send_sems, recv_sems):
    rows, channels = x_ref.shape
    tap_count, group_count = mr_ref.shape[1:]
    per_group = channels // group_count
    groups = LANES // per_group
    half = rows // 2
    blocks = channels // LANES
    part = channels // CHUNKS
    outer, inner = axes
    inner_size = lax.axis_size(inner)
    count = lax.axis_size(outer) * inner_size
    me = lax.axis_index(outer) * inner_size + lax.axis_index(inner)
    behind, ahead = me - 1, me + 1
    has_behind, has_ahead = me > 0, me < count - 1

    def place(index):
        return (index // inner_size, index % inner_size)

    barrier = pltpu.get_barrier_semaphore()

    @pl.when(has_behind)
    def _():
        pl.semaphore_signal(barrier, inc=1, device_id=place(behind), device_id_type=MESH)

    @pl.when(has_ahead)
    def _():
        pl.semaphore_signal(barrier, inc=1, device_id=place(ahead), device_id_type=MESH)

    peers = has_behind.astype(jnp.int32) + has_ahead.astype(jnp.int32)
    pl.semaphore_wait(barrier, peers)

    def lead_copy():
        return pltpu.make_async_remote_copy(
            src_ref=x_ref.at[pl.ds(rows - LEAD, LEAD)], dst_ref=lead_ref,
            send_sem=lead_sems.at[0], recv_sem=lead_sems.at[1],
            device_id=place(ahead), device_id_type=MESH)

    def part_copy(k):
        cs = lanes_of(k, part)
        return pltpu.make_async_remote_copy(
            src_ref=win_ref.at[pl.ds(rows, tap_count), cs],
            dst_ref=win_ref.at[pl.ds(0, tap_count), cs],
            send_sem=send_sems.at[k], recv_sem=recv_sems.at[k],
            device_id=place(ahead), device_id_type=MESH)

    tail = tap_count + LEAD

    def tell_copy():
        return pltpu.make_async_remote_copy(
            src_ref=tell_ref, dst_ref=told_ref,
            send_sem=lead_sems.at[2], recv_sem=lead_sems.at[3],
            device_id=place(ahead), device_id_type=MESH)

    def early_copy(k):
        cs = lanes_of(k, part)
        return pltpu.make_async_remote_copy(
            src_ref=give_ref.at[:, cs], dst_ref=got_ref.at[:, cs],
            send_sem=send_sems.at[k], recv_sem=recv_sems.at[k],
            device_id=place(ahead), device_id_type=MESH)

    @pl.when(has_ahead)
    def _():
        lead_copy().start()

    z_ref[...] = jnp.zeros_like(z_ref)
    w_ref[...] = jnp.zeros_like(w_ref)
    share = (gain_ref, feat_ref, taps_ref, h_ref, z_ref, w_ref, s_ref, sum_ref)
    here = blocks // CHUNKS
    early_blocks = EARLY * here

    def mr_product(taps, first, size):
        return (stream(z_ref, taps[1], first, size) * stream(z_ref, taps[2], first, size)).astype(BF16)

    def mr_taps_of(cs):
        return feat_rows(feat_ref, 1, gain_ref[0, 1:2, cs], cs)

    first_tail = rows - tail
    read_tail = lambda c: x_ref[first_tail:, lanes_of(c)]
    s_ref[:tail] = row_scale(square_sums(read_tail, tail, blocks), channels)
    sum_ref[:tail] = jnp.zeros((tail, LANES), F32)
    start_tail = LEAD + first_tail

    @pl.loop(0, CHUNKS)
    def _(k):
        @pl.loop(0, here)
        def _(b):
            c = k * here + b
            short_block(c, read_tail, tail, start_tail, *share)

            @pl.when(k < EARLY)
            def _():
                give_ref[:, lanes_of(c)] = h_ref[start_tail : start_tail + tail, lanes_of(c)].astype(BF16)

        @pl.when(has_ahead & (k > 0) & (k <= EARLY))
        def _():
            early_copy(k - 1).start()

    scale_ref[start_tail : start_tail + tail] = row_scale(sum_ref[:tail], channels)
    tell_ref[...] = scale_ref[start_tail : start_tail + tail]
    first_sent = rows - tap_count

    @pl.loop(EARLY, CHUNKS)
    def _(k):
        @pl.loop(0, here)
        def _(b):
            cs = lanes_of(k * here + b)
            taps = mr_taps_of(cs)
            n = tap_count + 8
            top = LEAD + first_sent - 8
            z_ref[0:n] = h_ref[top : top + n, cs] * scale_ref[top : top + n]
            for first, size in pieces(tap_count):
                win_ref[rows + first : rows + first + size, cs] = mr_product(taps, first, size)

        @pl.when(has_ahead & (k == EARLY))
        def _():
            tell_copy().start()

        @pl.when(has_ahead & (k > EARLY))
        def _():
            part_copy(k - 1).start()

    at_tap = lax.broadcasted_iota(jnp.int32, (tap_count, tap_count), 0)
    at_lag = lax.broadcasted_iota(jnp.int32, (tap_count, tap_count), 1)
    flip = jnp.where((at_tap + at_lag == tap_count) | (at_tap + at_lag == 0), 1.0, 0.0).astype(BF16)
    past = (lax.broadcasted_iota(jnp.int32, (half, tap_count), 1)
            > lax.broadcasted_iota(jnp.int32, (half, tap_count), 0))
    base_ref[...] = lax.dot_general(mr_ref[0], flip, (((0,), (0,)), ((), ())),
                                    preferred_element_type=F32)
    rhs_ref[...] = jnp.zeros_like(rhs_ref)

    @pl.when(has_ahead)
    def _():
        part_copy(CHUNKS - 1).start()

    @pl.when(has_behind)
    def _():
        lead_copy().wait_recv()

    @pl.when(jnp.logical_not(has_behind))
    def _():
        lead_ref[...] = jnp.zeros_like(lead_ref)
        win_ref[:tap_count] = jnp.zeros((tap_count, channels), BF16)

    head = LEAD + first_sent
    z_ref[0:8] = jnp.zeros((8, LANES), F32)
    read_head = lambda c: jnp.concatenate(
        [lead_ref[:, lanes_of(c)], x_ref[:first_sent, lanes_of(c)]], axis=0)
    s_ref[:head] = row_scale(square_sums(read_head, head, blocks), channels)
    sum_ref[:head] = jnp.zeros((head, LANES), F32)

    @pl.loop(0, blocks)
    def _(c):
        short_block(c, read_head, head, 0, *share)

    scale_ref[:head] = row_scale(sum_ref[:head], channels)

    @pl.loop(0, blocks)
    def _(c):
        cs = lanes_of(c)
        taps = mr_taps_of(cs)
        z_ref[0 : rows + 8] = h_ref[LEAD - 8 :, cs] * scale_ref[LEAD - 8 :]

        def put(low, high):
            for first, size in pieces(high - low):
                first += low
                win_ref[tap_count + first : tap_count + first + size, cs] = mr_product(taps, first, size)

        put(0, first_sent)

        @pl.when(c < early_blocks)
        def _():
            put(first_sent, rows)

        for first, size in pieces(rows):
            u_ref[first : first + size, cs] = stream(z_ref, taps[0], first, size)

    @pl.loop(0, blocks)
    def _(c):
        lags = base_ref[pl.ds(pl.multiple_of(c * groups, groups), groups), :]
        for g in range(groups):
            row = jnp.broadcast_to(lags[g : g + 1], (half, tap_count))
            turned = pltpu.roll(row, 0, 1, stride=1, stride_axis=0)
            gs = slice(g * half, (g + 1) * half)
            table_ref[c, gs, :tap_count] = jnp.where(past, turned, 0.0).astype(BF16)
            table_ref[c, gs, tap_count:] = jnp.where(past, 0.0, turned).astype(BF16)

    lane_group = lax.broadcasted_iota(jnp.int32, (half, LANES), 1) // per_group
    reach = half + tap_count

    @pl.loop(0, CHUNKS)
    def _(k):
        @pl.when(has_behind & (k == 0))
        def _():
            tell_copy().wait_recv()

        @pl.when(has_behind & (k < EARLY))
        def _():
            early_copy(k).wait_recv()

            @pl.loop(0, here)
            def _(b):
                cs = lanes_of(k * here + b)
                taps = mr_taps_of(cs)
                z_ref[0:tail] = got_ref[:, cs].astype(F32) * told_ref[...]
                for first, size in pieces(tap_count):
                    win_ref[first : first + size, cs] = mr_product(taps, tail - tap_count - 8 + first, size)

        @pl.when(has_behind & (k >= EARLY))
        def _():
            part_copy(k).wait_recv()

        @pl.loop(0, blocks // CHUNKS, step=STEP)
        def _(b):
          for slot in range(STEP):
            c = k * (blocks // CHUNKS) + b + slot
            cs = lanes_of(c)
            rhs_ref[slot, :reach, :LANES] = win_ref[:reach, cs]
            rhs_ref[slot, :reach, LANES:] = win_ref[half : half + reach, cs]
            product = jnp.dot(table_ref[c], rhs_ref[slot], preferred_element_type=F32)
            for side in range(2):
                ls = slice(side * LANES, (side + 1) * LANES)
                f = product[0:half, ls]
                for g in range(1, groups):
                    f = jnp.where(lane_group == g, product[g * half : (g + 1) * half, ls], f)
                rs = slice(side * half, (side + 1) * half)
                hs = slice(LEAD + side * half, LEAD + (side + 1) * half)
                out_ref[rs, cs] = (h_ref[hs, cs] + u_ref[rs, cs] * f).astype(BF16)

    @pl.when(has_ahead)
    def _():
        lead_copy().wait_send()

        tell_copy().wait_send()

        @pl.loop(0, EARLY)
        def _(k):
            early_copy(k).wait_send()

        @pl.loop(EARLY, CHUNKS)
        def _(k):
            part_copy(k).wait_send()


def on_device(axes, tokens, norm_gain, feat_taps, se_taps, mr_taps):
    rows, channels = tokens.shape
    tap_count, group_count = mr_taps.shape[1:]
    groups = LANES * group_count // channels
    blocks = channels // LANES
    spread = 2 * tap_count
    return pl.pallas_call(
        functools.partial(kernel, axes),
        out_shape=jax.ShapeDtypeStruct((rows, channels), BF16),
        in_specs=[pl.BlockSpec(memory_space=pltpu.VMEM)] * 5,
        out_specs=pl.BlockSpec(memory_space=pltpu.VMEM),
        scratch_shapes=[
            pltpu.VMEM((LEAD, channels), BF16),
            pltpu.VMEM((tap_count + rows, channels), BF16),
            pltpu.VMEM((LEAD + rows, channels), F32),
            pltpu.VMEM((rows, channels), F32),
            pltpu.VMEM((blocks, groups * rows // 2, spread), BF16),
            pltpu.VMEM((group_count, tap_count), F32),
            pltpu.VMEM((STEP, spread, 2 * LANES), BF16),
            pltpu.VMEM((LEAD + rows, LANES), F32),
            pltpu.VMEM((LEAD + rows, LANES), F32),
            pltpu.VMEM((LEAD + rows, LANES), F32),
            pltpu.VMEM((LEAD + rows, LANES), F32),
            pltpu.VMEM((LEAD + rows, LANES), F32),
            pltpu.VMEM((tap_count + LEAD, LANES), F32),
            pltpu.VMEM((tap_count + LEAD, LANES), F32),
            pltpu.VMEM((tap_count + LEAD, EARLY * channels // CHUNKS), BF16),
            pltpu.VMEM((tap_count + LEAD, EARLY * channels // CHUNKS), BF16),
            pltpu.SemaphoreType.DMA((4,)),
            pltpu.SemaphoreType.DMA((CHUNKS,)),
            pltpu.SemaphoreType.DMA((CHUNKS,)),
        ],
        compiler_params=pltpu.CompilerParams(
            collective_id=0, has_side_effects=True, vmem_limit_bytes=67043328),
        name="pair",
    )(tokens, norm_gain, feat_taps.transpose(0, 2, 3, 1, 4), se_taps.transpose(1, 0, 2), mr_taps)


def solution(mesh):
    axes = tuple(mesh.axis_names)
    placed = (P(axes, None), P(), P(), P(), P())
    return jax.shard_map(
        functools.partial(on_device, axes),
        mesh=mesh,
        in_specs=placed,
        out_specs=P(axes, None),
        check_vma=False,
    )
```
